32 devices in a mesh: rows: 4 (over y, core), cols: 8 (over z, x).
Axes of the slice: x: 2, y: 2, z: 4, core: 2. Of those that a mesh axis runs over, the one named last changes fastest.
Arguments:
- object_field: float32 [2, 512, 1024], P(None, 'rows', 'cols'), may hold values from -6 to 6
- probe: float32 [2, 256, 256], replicated, may hold values from -6 to 6
- amplitudes: float32 [4, 8, 4, 256, 256], P('rows', 'cols'), may hold values from 0.5 to 4
- offsets: int32 [4, 8, 4, 2], P('rows', 'cols'), may hold values from 0 to 128
Outputs:
- updated: float32 [2, 512, 1024], P(None, 'rows', 'cols')
The draws below stay inside these ranges and needn't reach their ends.
Inputs may be any that keep to these rules, and one draw needn't show every extreme that they name: `offsets`: every window lies inside its tile's extended region of 384 cells a side.
All inputs are finite; a program needn't handle non-finite values.
Results may differ from the reference program's by a relative error of at most 0.0001.
Values sent between devices are 32-bit elements; how exact they have to be, the bound alone decides.
No kernel may reach another device: no remote copies, remote signals or barrier semaphores. Data moves between devices by JAX's collectives and lax.ppermute only.
A program may use at most 64 MiB of HBM per device.

```python
import math
import jax
import jax.numpy as jnp
from jax import lax

OWN = 128
WIN = 256
POS = 4
ITERS = 2
TR = 4
TC = 8
NR = 512
NC = 1024


def set_ends(values, stream_key, low, high):
    spot = [jax.random.randint(jax.random.fold_in(stream_key, axis), (), 0, length) for axis, length in enumerate(values.shape)]
    longest = values.shape.index(max(values.shape))
    next_to = spot[:longest] + [(spot[longest] + 1) % values.shape[longest]] + spot[longest + 1:]
    return values.at[tuple(spot)].set(low).at[tuple(next_to)].set(high)


def level_of(rng, shape, pieces, low, largest):
    factor_of = 1.0
    for position, blocks in pieces:
        draws = jax.random.uniform(jax.random.fold_in(jax.random.fold_in(rng, 6), position), (blocks,), jnp.float32, low / len(pieces), largest / len(pieces))
        factor_of = factor_of * jnp.repeat(jnp.exp(draws), shape[position] // blocks).reshape((-1,) + (1,) * (len(shape) - 1 - position))
    return factor_of


def scatter_about(key, extent, deviation, most, split=(), kind=jnp.bfloat16):
    entries = jax.random.normal(key, extent, jnp.float32) * deviation
    if len(split) > 0:
        entries = level_of(key, extent, split, -0.22, 0.18) * entries
    return jnp.clip(entries, min=-most, max=most).astype(kind)


def setup_inputs(seed: int = 0) -> dict:
    key_list = jax.random.split(jax.random.key(seed), 5)
    return {
        "object_field": scatter_about(key_list[0], (2, NR, NC), 1.0, 6.0, ((1, 4), (2, 8)), jnp.float32),
        "probe": scatter_about(key_list[1], (2, WIN, WIN), 1.0, 6.0, (), jnp.float32),
        "amplitudes": jnp.clip(jnp.exp(math.log(4.0) - 2.0794415 * jax.random.uniform(key_list[2], (TR, TC, POS, WIN, WIN), jnp.float32) ** level_of(key_list[2], (TR, TC, POS, WIN, WIN), ((0, 4), (1, 8)), -0.2, 0.2)), 0.5, 4.0),
        "offsets": set_ends(jax.random.randint(key_list[3], (TR, TC, POS, 2), 0, 3 * OWN - WIN + 1), jax.random.fold_in(key_list[3], 1), 0, 3 * OWN - WIN).astype(jnp.int32),
    }


floor_level = 0.5

def window_term(window, probe, amp):
    pr, pi = (probe[0], probe[1])
    orr, oi = (window[0], window[1])
    er = pr * orr - pi * oi
    ei = pr * oi + pi * orr
    far = jnp.fft.fft2(er + 1j * ei, norm='ortho')
    fr = jnp.real(far)
    fi = jnp.imag(far)
    modulus = jnp.sqrt(fr * fr + fi * fi)
    keep = 1.0 - amp / jnp.maximum(modulus, floor_level)
    back = jnp.fft.ifft2(fr * keep + 1j * (fi * keep), norm='ortho')
    br = jnp.real(back)
    bi = jnp.imag(back)
    return jnp.stack([pr * br + pi * bi, pr * bi - pi * br])

def reference(object_field, probe, amplitudes, offsets):
    count = TR * TC * POS
    index = jnp.arange(count, dtype=jnp.int32)
    tile_row = index // (TC * POS)
    tile_col = index // POS % TC
    starts = offsets.reshape(count, 2).astype(jnp.int32)
    first = tile_row * OWN + starts[:, 0]
    second = tile_col * OWN + starts[:, 1]
    amps = amplitudes.reshape(count, WIN, WIN)
    zero = jnp.zeros((), jnp.int32)
    power = (probe[0] * probe[0] + probe[1] * probe[1])[None]

    def light_step(acc, item):
        y0, x0 = item
        cur = lax.dynamic_slice(acc, (zero, y0, x0), (1, WIN, WIN))
        return (lax.dynamic_update_slice(acc, cur + power, (zero, y0, x0)), None)
    light = jnp.zeros((1, NR + 2 * OWN, NC + 2 * OWN), jnp.float32)
    light, _ = lax.scan(light_step, light, (first, second))
    illumination = light[:, OWN:OWN + NR, OWN:OWN + NC]
    field = object_field
    for step in range(ITERS):
        padded = jnp.pad(field, ((0, 0), (OWN, OWN), (OWN, OWN)))

        def grad_step(acc, item):
            y0, x0, amp = item
            window = lax.dynamic_slice(padded, (zero, y0, x0), (2, WIN, WIN))
            term = window_term(window, probe, amp)
            cur = lax.dynamic_slice(acc, (zero, y0, x0), (2, WIN, WIN))
            return (lax.dynamic_update_slice(acc, cur + term, (zero, y0, x0)), None)
        acc = jnp.zeros((2, NR + 2 * OWN, NC + 2 * OWN), jnp.float32)
        acc, _ = lax.scan(grad_step, acc, (first, second, amps))
        gradient = acc[:, OWN:OWN + NR, OWN:OWN + NC]
        field = field - gradient / (illumination + 1.0)
    return field
```

```python
import functools
import math

import jax
import jax.numpy as jnp
import numpy as np
from jax import lax
from jax.experimental import pallas as pl
from jax.experimental.pallas import tpu as pltpu
from jax.sharding import PartitionSpec as P

ITERS = 2
FLOOR = 0.5
f32 = jnp.float32
bf16 = jnp.bfloat16
VMEM = pl.BlockSpec(memory_space=pltpu.VMEM)
SMEM = pl.BlockSpec(memory_space=pltpu.SMEM)


def swap(value, axis, odd):
    n = lax.axis_size(axis)
    first = 1 if odd else 0
    pairs = []
    for i in range(first, n - 1, 2):
        pairs += [(i, i + 1), (i + 1, i)]
    return lax.ppermute(value, axis, pairs)


def dft_matrices(size):
    half = size // 2
    k = np.arange(half)[:, None]
    m = np.arange(half)[None, :]
    mats = []
    for odd in (0, 1):
        angle = 2.0 * np.pi / size * (((2 * k + odd) * m) % size)
        c = np.cos(angle) / math.sqrt(size)
        s = np.sin(angle) / math.sqrt(size)
        w = np.block([[c, s], [-s, c]])
        mats += [w, w.T]
    mats = np.stack(mats).astype(np.float32)
    hi = mats.astype(jnp.bfloat16)
    lo = (mats - hi.astype(np.float32)).astype(jnp.bfloat16)
    return np.stack([hi, lo])


def split(x):
    hi = x.astype(bf16)
    lo = (x - hi.astype(f32)).astype(bf16)
    return hi, lo


def times_right(x, mats, which):
    hi, lo = split(x)
    lhs = jnp.concatenate([hi, lo, hi], 1)
    rhs = jnp.concatenate([mats[0, which], mats[0, which], mats[1, which]], 0)
    return jnp.dot(lhs, rhs, preferred_element_type=f32)


def times_left(mats, which, x):
    hi, lo = split(x)
    lhs = jnp.concatenate([mats[0, which], mats[1, which], mats[0, which]], 1)
    rhs = jnp.concatenate([hi, hi, lo], 0)
    return jnp.dot(lhs, rhs, preferred_element_type=f32)


WE, WET, WO, WOT = 0, 1, 2, 3


def split_three(x):
    a = x.astype(bf16)
    rest = x - a.astype(f32)
    b = rest.astype(bf16)
    return [a, b, (rest - b.astype(f32)).astype(bf16)]


def amps_kernel(amps_ref, perm_ref, out_ref):
    perm = perm_ref[0]
    perm_t = perm_ref[1]
    for p in range(amps_ref.shape[0]):
        cols = jnp.dot(
            jnp.concatenate(split_three(amps_ref[p]), 1),
            jnp.concatenate([perm] * 3, 0),
            preferred_element_type=f32,
        )
        out_ref[p] = jnp.dot(
            jnp.concatenate([perm_t] * 3, 1),
            jnp.concatenate(split_three(cols), 0),
            preferred_element_type=f32,
        )


def place_at(x, shift, extent):
    rows = x.shape[0]
    wide = jnp.concatenate([x, jnp.zeros((rows, extent - x.shape[1]), f32)], 1)
    return pltpu.roll(wide, shift, 1)


def windows_kernel(
    with_light, flags_ref, offs_ref, strip_ref, even_ref, odd_ref, probe_ref, amps_ref,
    mats_ref, mid_ref, to_even_ref, to_odd_ref, ext, acc,
):
    own = strip_ref.shape[1]
    extent = 3 * own
    size = probe_ref.shape[1]
    half = size // 2
    positions = amps_ref.shape[0]
    parity = flags_ref[0]
    even_at = pl.multiple_of((1 - parity) * 2 * own, own)
    odd_at = pl.multiple_of(parity * 2 * own, own)
    for k in range(2):
        for j in range(3):
            lanes = slice(j * own, (j + 1) * own)
            ext[3 * k + j, own : 2 * own, :] = strip_ref[k, :, lanes]
            ext[3 * k + j, pl.ds(even_at, own), :] = even_ref[k, :, lanes]
            ext[3 * k + j, pl.ds(odd_at, own), :] = odd_ref[k, :, lanes]
    acc[...] = jnp.zeros_like(acc)
    mats = mats_ref

    def window_of(k, rows, back_by):
        wide = jnp.concatenate([ext[3 * k + j, rows, :] for j in range(3)], 1)
        return pltpu.roll(wide, back_by, 1)[:, :size]

    def add_at(k, rows, x, shift):
        wide = place_at(x, shift, extent)
        for j in range(3):
            acc[3 * k + j, rows, :] += wide[:, j * own : (j + 1) * own]

    def window(p):
        first = offs_ref[2 * p]
        second = offs_ref[2 * p + 1]
        back_by = jnp.where(second == 0, 0, extent - second)
        parts = []
        for h in (0, 1):
            rows = pl.ds(first + h * half, half)
            orr = window_of(0, rows, back_by)
            oi = window_of(1, rows, back_by)
            pr = probe_ref[0, h * half : (h + 1) * half, :]
            pi = probe_ref[1, h * half : (h + 1) * half, :]
            er = pr * orr - pi * oi
            ei = pr * oi + pi * orr
            s = jnp.concatenate([er[:, :half] + er[:, half:], ei[:, :half] + ei[:, half:]], 1)
            d = jnp.concatenate([er[:, :half] - er[:, half:], ei[:, :half] - ei[:, half:]], 1)
            parts.append((times_right(s, mats, WET), times_right(d, mats, WOT)))
        (te, to), (be, bo) = parts
        e_out = None
        outs = []
        for odd, (e, o) in enumerate(((te + be, to + bo), (te - be, to - bo))):
            x = jnp.concatenate(
                [
                    jnp.concatenate([e[:, :half], o[:, :half]], 1),
                    jnp.concatenate([e[:, half:], o[:, half:]], 1),
                ],
                0,
            )
            far = times_left(mats, WO if odd else WE, x)
            fr = far[:half]
            fi = far[half:]
            amp = amps_ref[p, odd * half : (odd + 1) * half, :]
            keep = 1.0 - amp * lax.rsqrt(jnp.maximum(fr * fr + fi * fi, FLOOR * FLOOR))
            y = jnp.concatenate([fr * keep, fi * keep], 0)
            outs.append(times_left(mats, WOT if odd else WET, y))
        e_out, o_out = outs
        for h in (0, 1):
            v = e_out + o_out if h == 0 else e_out - o_out
            le = jnp.concatenate([v[:half, :half], v[half:, :half]], 1)
            lo = jnp.concatenate([v[:half, half:], v[half:, half:]], 1)
            e = times_right(le, mats, WE)
            o = times_right(lo, mats, WO)
            u = e + o
            w = e - o
            br = jnp.concatenate([u[:, :half], w[:, :half]], 1)
            bi = jnp.concatenate([u[:, half:], w[:, half:]], 1)
            pr = probe_ref[0, h * half : (h + 1) * half, :]
            pi = probe_ref[1, h * half : (h + 1) * half, :]
            rows = pl.ds(first + h * half, half)
            add_at(0, rows, pr * br + pi * bi, second)
            add_at(1, rows, pr * bi - pi * br, second)
            if with_light:
                add_at(2, rows, pr * pr + pi * pi, second)

    for p in range(positions):
        window(p)
    for k in range(mid_ref.shape[0]):
        for j in range(3):
            lanes = slice(j * own, (j + 1) * own)
            mid_ref[k, :, lanes] = acc[3 * k + j, own : 2 * own, :]
            to_even_ref[k, :, lanes] = acc[3 * k + j, pl.ds(even_at, own), :]
            to_odd_ref[k, :, lanes] = acc[3 * k + j, pl.ds(odd_at, own), :]


def join_kernel(flags_ref, own_ref, even_ref, odd_ref, strip_ref):
    own = own_ref.shape[2]
    parity = flags_ref[1]
    strip_ref[:, :, own : 2 * own] = own_ref[...]

    @pl.when(parity == 0)
    def _():
        strip_ref[:, :, 2 * own :] = even_ref[...]
        strip_ref[:, :, :own] = odd_ref[...]

    @pl.when(parity == 1)
    def _():
        strip_ref[:, :, 2 * own :] = odd_ref[...]
        strip_ref[:, :, :own] = even_ref[...]


def rows_kernel(flags_ref, mid_ref, even_ref, odd_ref, keep_ref, to_even_ref, to_odd_ref):
    own = keep_ref.shape[2]
    parity = flags_ref[1]
    total = mid_ref[...] + even_ref[...] + odd_ref[...]
    keep_ref[...] = total[:, :, own : 2 * own]

    @pl.when(parity == 0)
    def _():
        to_even_ref[...] = total[:, :, 2 * own :]
        to_odd_ref[...] = total[:, :, :own]

    @pl.when(parity == 1)
    def _():
        to_even_ref[...] = total[:, :, :own]
        to_odd_ref[...] = total[:, :, 2 * own :]


def first_update_kernel(field_ref, keep_ref, even_ref, odd_ref, out_ref, light_ref):
    total = keep_ref[...] + even_ref[...] + odd_ref[...]
    light = total[2] + 1.0
    light_ref[...] = light
    out_ref[0] = field_ref[0] - total[0] / light
    out_ref[1] = field_ref[1] - total[1] / light


def update_kernel(field_ref, light_ref, keep_ref, even_ref, odd_ref, out_ref):
    total = keep_ref[...] + even_ref[...] + odd_ref[...]
    light = light_ref[...]
    out_ref[0] = field_ref[0] - total[0] / light
    out_ref[1] = field_ref[1] - total[1] / light


def call(kernel, shapes, specs, *args, scratch=(), flops=0):
    outs = [jax.ShapeDtypeStruct(s, f32) for s in shapes]
    moved = sum(a.size * a.dtype.itemsize for a in args)
    got = pl.pallas_call(
        kernel,
        out_shape=outs,
        in_specs=specs,
        out_specs=[VMEM] * len(outs),
        scratch_shapes=list(scratch),
        compiler_params=pltpu.CompilerParams(vmem_limit_bytes=40 * 2**20),
        cost_estimate=pl.CostEstimate(flops=flops, bytes_accessed=moved, transcendentals=0),
    )(*args)
    return got[0] if len(outs) == 1 else got


def local(object_field, probe, amplitudes, offsets):
    own = object_field.shape[1]
    size = probe.shape[1]
    positions = amplitudes.shape[2]
    extent = 3 * own
    amps = amplitudes.reshape(positions, size, size)
    offs = offsets.reshape(2 * positions)
    flags = jnp.stack([lax.axis_index("rows") % 2, lax.axis_index("cols") % 2]).astype(jnp.int32)
    mats = jnp.asarray(dft_matrices(size))
    order = np.concatenate([np.arange(0, size, 2), np.arange(1, size, 2)])
    perm = (np.arange(size)[:, None] == order[None, :]).astype(jnp.bfloat16)
    perm = jnp.asarray(np.stack([perm, perm.T]))
    amps = call(
        amps_kernel, [(positions, size, size)], [VMEM, VMEM], amps, perm,
        flops=6 * positions * size**3,
    )
    field = object_field
    light = None
    for step in range(ITERS):
        layers = 3 if step == 0 else 2
        strip = call(
            join_kernel, [(2, own, extent)], [SMEM] + [VMEM] * 3,
            flags, field, swap(field, "cols", False), swap(field, "cols", True),
        )
        mid, to_even, to_odd = call(
            functools.partial(windows_kernel, step == 0),
            [(layers, own, extent)] * 3,
            [SMEM, SMEM] + [VMEM] * 6,
            flags, offs, strip, swap(strip, "rows", False), swap(strip, "rows", True),
            probe, amps, mats,
            scratch=[pltpu.VMEM((3 * k, extent, own), f32) for k in (2, layers)],
            flops=48 * positions * size**3,
        )
        keep, to_even, to_odd = call(
            rows_kernel, [(layers, own, own)] * 3, [SMEM] + [VMEM] * 3,
            flags, mid, swap(to_even, "rows", False), swap(to_odd, "rows", True),
        )
        even, odd = swap(to_even, "cols", False), swap(to_odd, "cols", True)
        if step == 0:
            field, light = call(
                first_update_kernel, [(2, own, own), (own, own)], [VMEM] * 4,
                field, keep, even, odd,
            )
        else:
            field = call(
                update_kernel, [(2, own, own)], [VMEM] * 5, field, light, keep, even, odd
            )
    return field


def solution(mesh):
    placed = (
        P(None, "rows", "cols"),
        P(),
        P("rows", "cols", None, None, None),
        P("rows", "cols", None, None),
    )
    return jax.shard_map(
        local, mesh=mesh, in_specs=placed, out_specs=P(None, "rows", "cols"), check_vma=False
    )
```

```python
import math

import jax
import jax.numpy as jnp
import numpy as np
from jax import lax
from jax.experimental import pallas as pl
from jax.experimental.pallas import tpu as pltpu
from jax.sharding import PartitionSpec as P


ITERS = 2
FLOOR = 0.5
f32 = jnp.float32
bf16 = jnp.bfloat16
VMEM = pl.BlockSpec(memory_space=pltpu.VMEM)
SMEM = pl.BlockSpec(memory_space=pltpu.SMEM)


def mate(i, n, odd):
    other = ((i + 1) ^ 1) - 1 if odd else i ^ 1
    return other if 0 <= other < n else None


def swap(value, row=None, col=None):
    rows, cols = lax.axis_size("rows"), lax.axis_size("cols")
    far = 2 if cols % 4 == 0 else 1
    pairs = []
    for r in range(rows):
        for c in range(cols):
            to_r = r if row is None else mate(r, rows, row)
            to_c = c if col is None else mate(c, cols, col)
            if to_r is None:
                to_r, to_c = r, c ^ far
            elif to_c is None:
                to_r, to_c = (r ^ 1 if row is None else to_r), c
            pairs.append((r * cols + c, to_r * cols + to_c))
    return lax.ppermute(value, ("rows", "cols"), pairs)


def halo(tile):
    col_odd = swap(tile, col=1)
    col_even = swap(tile, col=0)
    odd_row = [swap(tile, row=1), swap(tile, row=1, col=0), swap(tile, row=1, col=1)]
    even_row = [swap(tile, row=0), swap(col_even, row=0), swap(col_odd, row=0)]
    return [tile, col_even, col_odd] + even_row + odd_row


def dft_matrices(size):
    half = size // 2
    k = np.arange(half)[:, None]
    m = np.arange(half)[None, :]
    mats = []
    for odd in (0, 1):
        angle = 2.0 * np.pi / size * (((2 * k + odd) * m) % size)
        c = np.cos(angle) / math.sqrt(size)
        s = np.sin(angle) / math.sqrt(size)
        w = np.block([[c, s], [-s, c]])
        mats += [w, w.T]
    mats = np.stack(mats).astype(np.float32)
    hi = mats.astype(jnp.bfloat16)
    lo = (mats - hi.astype(np.float32)).astype(jnp.bfloat16)
    return np.stack([hi, lo])


def split(x):
    hi = x.astype(bf16)
    lo = (x - hi.astype(f32)).astype(bf16)
    return hi, lo


def times_right(x, mats, which):
    hi, lo = split(x)
    lhs = jnp.concatenate([hi, lo, hi], 1)
    rhs = jnp.concatenate([mats[0, which], mats[0, which], mats[1, which]], 0)
    return jnp.dot(lhs, rhs, preferred_element_type=f32)


def times_left(mats, which, x):
    hi, lo = split(x)
    lhs = jnp.concatenate([mats[0, which], mats[1, which], mats[0, which]], 1)
    rhs = jnp.concatenate([hi, hi, lo], 0)
    return jnp.dot(lhs, rhs, preferred_element_type=f32)


WE, WET, WO, WOT = 0, 1, 2, 3


def split_three(x):
    a = x.astype(bf16)
    rest = x - a.astype(f32)
    b = rest.astype(bf16)
    return [a, b, (rest - b.astype(f32)).astype(bf16)]


def amps_kernel(amps_ref, perm_ref, out_ref):
    perm = perm_ref[0]
    perm_t = perm_ref[1]
    for p in range(amps_ref.shape[0]):
        cols = jnp.dot(
            jnp.concatenate(split_three(amps_ref[p]), 1),
            jnp.concatenate([perm] * 3, 0),
            preferred_element_type=f32,
        )
        out_ref[p] = jnp.dot(
            jnp.concatenate([perm_t] * 3, 1),
            jnp.concatenate(split_three(cols), 0),
            preferred_element_type=f32,
        )


def place_at(x, shift, extent):
    rows = x.shape[0]
    wide = jnp.concatenate([x, jnp.zeros((rows, extent - x.shape[1]), f32)], 1)
    return pltpu.roll(wide, shift, 1)


def is_there(flags_ref, g, m):
    if g == 2:
        both = flags_ref[2] * flags_ref[3] if m == 2 else flags_ref[2]
        return both > 0
    return flags_ref[3] > 0 if m == 2 else None


def windows_kernel(flags_ref, offs_ref, *refs):
    tiles = refs[:9]
    probe_ref, amps_ref, mats, mid_ref, to_even_ref, ro_ref, de_ref, do_ref, ext, acc = refs[9:]
    own = mid_ref.shape[1]
    extent = 3 * own
    size = probe_ref.shape[1]
    half = size // 2
    positions = amps_ref.shape[0]
    row_parity = flags_ref[0]
    col_parity = flags_ref[1]
    even_at = pl.multiple_of((1 - row_parity) * 2 * own, own)
    odd_at = pl.multiple_of(row_parity * 2 * own, own)
    even_chunk = 2 * (1 - col_parity)
    odd_chunk = 2 * col_parity
    for g, at in enumerate((own, even_at, odd_at)):
        for m, chunk in enumerate((1, even_chunk, odd_chunk)):
            there = is_there(flags_ref, g, m)
            for k in range(2):
                tile = tiles[3 * g + m][k * own : (k + 1) * own, :]
                if there is not None:
                    tile = jnp.where(there, tile, 0.0)
                ext[3 * k + chunk, pl.ds(at, own), :] = tile
    acc[...] = jnp.zeros_like(acc)

    def window_of(k, rows, back_by):
        wide = jnp.concatenate([ext[3 * k + j, rows, :] for j in range(3)], 1)
        return pltpu.roll(wide, back_by, 1)[:, :size]

    def add_at(k, rows, x, shift):
        wide = place_at(x, shift, extent)
        for j in range(3):
            acc[3 * k + j, rows, :] += wide[:, j * own : (j + 1) * own]

    def window(p):
        first = offs_ref[2 * p]
        second = offs_ref[2 * p + 1]
        back_by = jnp.where(second == 0, 0, extent - second)
        parts = []
        for h in (0, 1):
            rows = pl.ds(first + h * half, half)
            orr = window_of(0, rows, back_by)
            oi = window_of(1, rows, back_by)
            pr = probe_ref[0, h * half : (h + 1) * half, :]
            pi = probe_ref[1, h * half : (h + 1) * half, :]
            er = pr * orr - pi * oi
            ei = pr * oi + pi * orr
            s = jnp.concatenate([er[:, :half] + er[:, half:], ei[:, :half] + ei[:, half:]], 1)
            d = jnp.concatenate([er[:, :half] - er[:, half:], ei[:, :half] - ei[:, half:]], 1)
            parts.append((times_right(s, mats, WET), times_right(d, mats, WOT)))
        (te, to), (be, bo) = parts
        e_out = None
        outs = []
        for odd, (e, o) in enumerate(((te + be, to + bo), (te - be, to - bo))):
            x = jnp.concatenate(
                [
                    jnp.concatenate([e[:, :half], o[:, :half]], 1),
                    jnp.concatenate([e[:, half:], o[:, half:]], 1),
                ],
                0,
            )
            far = times_left(mats, WO if odd else WE, x)
            fr = far[:half]
            fi = far[half:]
            amp = amps_ref[p, odd * half : (odd + 1) * half, :]
            keep = 1.0 - amp * lax.rsqrt(jnp.maximum(fr * fr + fi * fi, FLOOR * FLOOR))
            y = jnp.concatenate([fr * keep, fi * keep], 0)
            outs.append(times_left(mats, WOT if odd else WET, y))
        e_out, o_out = outs
        for h in (0, 1):
            v = e_out + o_out if h == 0 else e_out - o_out
            le = jnp.concatenate([v[:half, :half], v[half:, :half]], 1)
            lo = jnp.concatenate([v[:half, half:], v[half:, half:]], 1)
            e = times_right(le, mats, WE)
            o = times_right(lo, mats, WO)
            u = e + o
            w = e - o
            br = jnp.concatenate([u[:, :half], w[:, :half]], 1)
            bi = jnp.concatenate([u[:, half:], w[:, half:]], 1)
            pr = probe_ref[0, h * half : (h + 1) * half, :]
            pi = probe_ref[1, h * half : (h + 1) * half, :]
            rows = pl.ds(first + h * half, half)
            add_at(0, rows, pr * br + pi * bi, second)
            add_at(1, rows, pr * bi - pi * br, second)

    for p in range(positions):
        window(p)
    for k in range(mid_ref.shape[0]):
        for j in range(3):
            lanes = slice(j * own, (j + 1) * own)
            mid_ref[k, :, lanes] = acc[3 * k + j, own : 2 * own, :]
            to_even_ref[k, :, lanes] = acc[3 * k + j, pl.ds(even_at, own), :]
        rows = slice(k * own, (k + 1) * own)
        for out, chunk in ((ro_ref, 1), (de_ref, even_chunk), (do_ref, odd_chunk)):
            out[rows, :] = acc[3 * k + chunk, pl.ds(odd_at, own), :]


def pack_kernel(offs_ref, field_ref, out_ref):
    own = field_ref.shape[1]
    for k in range(2):
        out_ref[k * own : (k + 1) * own, :] = field_ref[k]
    lanes = lax.broadcasted_iota(jnp.int32, (8, own), 1)
    row = jnp.zeros((8, own), jnp.int32)
    for j in range(offs_ref.shape[0]):
        row = jnp.where(lanes == j, offs_ref[j], row)
    out_ref[2 * own :, :] = row.astype(f32)


def light_kernel(flags_ref, offs_ref, probe_ref, light_ref, padded):
    own = light_ref.shape[0]
    size = probe_ref.shape[1]
    positions = offs_ref.shape[0] // 18
    padded[...] = jnp.zeros_like(padded)
    power = probe_ref[0] * probe_ref[0] + probe_ref[1] * probe_ref[1]
    for j in range(size // own):
        padded[1 + j, own : own + size, :] = power[:, j * own : (j + 1) * own]
    light_ref[...] = jnp.ones_like(light_ref)
    lanes = lax.broadcasted_iota(jnp.int32, (own, own), 1)
    row_step = (1 - 2 * flags_ref[0]) * own
    col_step = (1 - 2 * flags_ref[1]) * own
    for g, row in enumerate((0, row_step, -row_step)):
        for m, col in enumerate((0, col_step, -col_step)):
            for p in range(positions):
                at = 2 * ((3 * g + m) * positions + p)
                first = 2 * own - row - offs_ref[at]
                second = 2 * own - col - offs_ref[at + 1]

                there = is_there(flags_ref, g, m)

                @pl.when(True if there is None else there)
                def _():
                    chunk = second // own
                    by = second - chunk * own
                    back = jnp.where(by == 0, 0, own - by)
                    rows = pl.ds(first, own)
                    left = pltpu.roll(padded[chunk, rows, :], back, 1)
                    right = pltpu.roll(padded[chunk + 1, rows, :], back, 1)
                    light_ref[...] += jnp.where(lanes < own - by, left, right)


def rows_kernel(flags_ref, mid_ref, even_ref, keep_ref, to_even_ref, to_odd_ref):
    own = keep_ref.shape[1]
    col_parity = flags_ref[1]
    for k in range(2):
        rows = slice(k * own, (k + 1) * own)
        total = mid_ref[k] + even_ref[k]
        left, right = total[:, :own], total[:, 2 * own :]
        keep_ref[rows, :] = total[:, own : 2 * own]
        to_even_ref[rows, :] = jnp.where(col_parity == 0, right, left)
        to_odd_ref[rows, :] = jnp.where(col_parity == 0, left, right)


def update_kernel(
    flags_ref, field_ref, light_ref, keep_ref, ce_ref, co_ref, ro_ref, de_ref, do_ref, out_ref
):
    own = light_ref.shape[0]
    row_ok, col_ok = flags_ref[2] > 0, flags_ref[3] > 0
    light = light_ref[...]
    for k in range(2):
        rows = slice(k * own, (k + 1) * own)
        total = keep_ref[rows, :] + ce_ref[rows, :]
        total += jnp.where(col_ok, co_ref[rows, :], 0.0)
        odd_row = ro_ref[rows, :] + de_ref[rows, :] + jnp.where(col_ok, do_ref[rows, :], 0.0)
        total += jnp.where(row_ok, odd_row, 0.0)
        out_ref[rows, :] = field_ref[rows, :] - total / light


def call(kernel, shapes, specs, *args, scratch=(), flops=0):
    outs = [jax.ShapeDtypeStruct(s, f32) for s in shapes]
    moved = sum(a.size * a.dtype.itemsize for a in args)
    got = pl.pallas_call(
        kernel,
        out_shape=outs,
        in_specs=specs,
        out_specs=[VMEM] * len(outs),
        scratch_shapes=list(scratch),
        compiler_params=pltpu.CompilerParams(vmem_limit_bytes=40 * 2**20),
        cost_estimate=pl.CostEstimate(flops=flops, bytes_accessed=moved, transcendentals=0),
    )(*args)
    return got[0] if len(outs) == 1 else got


def local(object_field, probe, amplitudes, offsets):
    own = object_field.shape[1]
    size = probe.shape[1]
    positions = amplitudes.shape[2]
    extent = 3 * own
    amps = amplitudes.reshape(positions, size, size)
    offs = offsets.reshape(2 * positions)
    row, col = lax.axis_index("rows"), lax.axis_index("cols")
    inner = [
        (at > 0) & (at < lax.axis_size(axis) - 1) for axis, at in (("rows", row), ("cols", col))
    ]
    flags = jnp.stack([row % 2, col % 2] + [x.astype(row.dtype) for x in inner]).astype(jnp.int32)
    mats = jnp.asarray(dft_matrices(size))
    order = np.concatenate([np.arange(0, size, 2), np.arange(1, size, 2)])
    perm = (np.arange(size)[:, None] == order[None, :]).astype(jnp.bfloat16)
    perm = jnp.asarray(np.stack([perm, perm.T]))
    amps = call(
        amps_kernel, [(positions, size, size)], [VMEM, VMEM], amps, perm,
        flops=6 * positions * size**3,
    )
    field = call(
        pack_kernel, [(2 * own + 8, own)], [SMEM, VMEM], offs, object_field
    )
    tiles = halo(field)
    around = jnp.concatenate([t[2 * own, : 2 * positions] for t in tiles]).astype(jnp.int32)
    light = call(
        light_kernel, [(own, own)], [SMEM, SMEM, VMEM], flags, around, probe,
        scratch=[pltpu.VMEM((2 + size // own + 1, size + 2 * own, own), f32)],
        flops=4 * positions * size**3,
    )
    for step in range(ITERS):
        if step > 0:
            tiles = halo(field)
        mid, to_even, ro, de, do = call(
            windows_kernel,
            [(2, own, extent)] * 2 + [(2 * own, own)] * 3,
            [SMEM, SMEM] + [VMEM] * 12,
            flags, offs, *tiles, probe, amps, mats,
            scratch=[pltpu.VMEM((6, extent, own), f32)] * 2,
            flops=48 * positions * size**3,
        )
        even = swap(to_even, row=0)
        odd_row = [swap(ro, row=1), swap(de, row=1, col=0), swap(do, row=1, col=1)]
        keep, to_even, to_odd = call(
            rows_kernel, [(2 * own, own)] * 3, [SMEM] + [VMEM] * 2, flags, mid, even
        )
        co, ce = swap(to_odd, col=1), swap(to_even, col=0)
        field = call(
            update_kernel, [(2 * own, own)], [SMEM] + [VMEM] * 8,
            flags, field, light, keep, ce, co, *odd_row,
        )
    return field.reshape(2, own, own)


def solution(mesh):
    placed = (
        P(None, "rows", "cols"),
        P(),
        P("rows", "cols", None, None, None),
        P("rows", "cols", None, None),
    )

    return jax.shard_map(
        local, mesh=mesh, in_specs=placed, out_specs=P(None, "rows", "cols"), check_vma=False
    )
```

```python
import math

import jax
import jax.numpy as jnp
import numpy as np
from jax import lax
from jax.experimental import pallas as pl
from jax.experimental.pallas import tpu as pltpu
from jax.sharding import PartitionSpec as P


ITERS = 2
FLOOR = 0.5
GROUP = 4
f32 = jnp.float32
bf16 = jnp.bfloat16
VMEM = pl.BlockSpec(memory_space=pltpu.VMEM)
SMEM = pl.BlockSpec(memory_space=pltpu.SMEM)


def mate(i, n, odd):
    other = ((i + 1) ^ 1) - 1 if odd else i ^ 1
    return other if 0 <= other < n else None


def swap(value, row=None, col=None):
    rows, cols = lax.axis_size("rows"), lax.axis_size("cols")
    far = 2 if cols % 4 == 0 else 1
    pairs = []
    for r in range(rows):
        for c in range(cols):
            to_r = r if row is None else mate(r, rows, row)
            to_c = c if col is None else mate(c, cols, col)
            if to_r is None:
                to_r, to_c = (r, c ^ far) if col == 0 else (rows - 1 - r, c)
            elif to_c is None:
                to_r, to_c = (r ^ 1 if row is None else to_r), c
            pairs.append((r * cols + c, to_r * cols + to_c))
    return lax.ppermute(value, ("rows", "cols"), pairs)


def halo(tile):
    col_odd = swap(tile, col=1)
    col_even = swap(tile, col=0)
    odd_row = [swap(tile, row=1), swap(tile, row=1, col=0), swap(tile, row=1, col=1)]
    even_row = [swap(tile, row=0), swap(col_even, row=0), swap(col_odd, row=0)]
    return [tile, col_even, col_odd] + even_row + odd_row


def dft_matrices(size):
    half = size // 2
    k = np.arange(half)[:, None]
    m = np.arange(half)[None, :]
    mats = []
    for odd in (0, 1):
        angle = 2.0 * np.pi / size * (((2 * k + odd) * m) % size)
        c = np.cos(angle) / math.sqrt(size)
        s = np.sin(angle) / math.sqrt(size)
        w = np.block([[c, s], [-s, c]])
        mats += [w, w.T]
    mats = np.stack(mats).astype(np.float32)
    hi = mats.astype(jnp.bfloat16)
    lo = (mats - hi.astype(np.float32)).astype(jnp.bfloat16)
    return np.stack([hi, lo])


def split(x):
    hi = x.astype(bf16)
    lo = (x - hi.astype(f32)).astype(bf16)
    return hi, lo


def times_right(x, mats, which):
    hi, lo = split(x)
    lhs = jnp.concatenate([hi, lo, hi], 1)
    rhs = jnp.concatenate([mats[0, which], mats[0, which], mats[1, which]], 0)
    return jnp.dot(lhs, rhs, preferred_element_type=f32)


def times_left(mats, which, x):
    hi, lo = split(x)
    lhs = jnp.concatenate([mats[0, which], mats[1, which], mats[0, which]], 1)
    rhs = jnp.concatenate([hi, hi, lo], 0)
    return jnp.dot(lhs, rhs, preferred_element_type=f32)


WE, WET, WO, WOT = 0, 1, 2, 3


def split_three(x):
    a = x.astype(bf16)
    rest = x - a.astype(f32)
    b = rest.astype(bf16)
    return [a, b, (rest - b.astype(f32)).astype(bf16)]


def amps_kernel(amps_ref, perm_ref, out_ref):
    perm = perm_ref[0]
    perm_t = perm_ref[1]
    for p in range(amps_ref.shape[0]):
        cols = jnp.dot(
            jnp.concatenate(split_three(amps_ref[p]), 1),
            jnp.concatenate([perm] * 3, 0),
            preferred_element_type=f32,
        )
        out_ref[p] = jnp.dot(
            jnp.concatenate([perm_t] * 3, 1),
            jnp.concatenate(split_three(cols), 0),
            preferred_element_type=f32,
        )


def place_at(x, shift, extent):
    rows = x.shape[0]
    wide = jnp.concatenate([x, jnp.zeros((rows, extent - x.shape[1]), f32)], 1)
    return pltpu.roll(wide, shift, 1)


def is_there(flags_ref, g, m):
    if g == 2:
        both = flags_ref[2] * flags_ref[3] if m == 2 else flags_ref[2]
        return both > 0
    return flags_ref[3] > 0 if m == 2 else None


def windows_kernel(flags_ref, offs_ref, *refs):
    tiles = refs[:9]
    probe_ref, amps_ref, mats, mid_ref, to_even_ref, ro_ref, de_ref, do_ref, ext, acc = refs[9:]
    own = mid_ref.shape[1]
    extent = 3 * own
    size = probe_ref.shape[1]
    half = size // 2
    positions = amps_ref.shape[0]
    row_parity = flags_ref[0]
    col_parity = flags_ref[1]
    even_at = pl.multiple_of((1 - row_parity) * 2 * own, own)
    odd_at = pl.multiple_of(row_parity * 2 * own, own)
    even_chunk = 2 * (1 - col_parity)
    odd_chunk = 2 * col_parity
    for g, at in enumerate((own, even_at, odd_at)):
        for m, chunk in enumerate((1, even_chunk, odd_chunk)):
            there = is_there(flags_ref, g, m)
            for k in range(2):
                tile = tiles[3 * g + m][k * own : (k + 1) * own, :]
                if there is not None:
                    tile = jnp.where(there, tile, 0.0)
                ext[3 * k + chunk, pl.ds(at, own), :] = tile
    acc[...] = jnp.zeros_like(acc)

    def window_of(k, rows, back_by):
        wide = jnp.concatenate([ext[3 * k + j, rows, :] for j in range(3)], 1)
        return pltpu.roll(wide, back_by, 1)[:, :size]

    def add_at(k, rows, x, shift):
        wide = place_at(x, shift, extent)
        for j in range(3):
            acc[3 * k + j, rows, :] += wide[:, j * own : (j + 1) * own]

    def halves(x):
        return [x[i * half : (i + 1) * half] for i in range(x.shape[0] // half)]

    def exits(p):
        first, second = offs_ref[0, p], offs_ref[1, p]
        back_by = jnp.where(second == 0, 0, extent - second)
        sums, differences = [], []
        for h in (0, 1):
            rows = pl.ds(first + h * half, half)
            orr = window_of(0, rows, back_by)
            oi = window_of(1, rows, back_by)
            pr = probe_ref[0, h * half : (h + 1) * half, :]
            pi = probe_ref[1, h * half : (h + 1) * half, :]
            er = pr * orr - pi * oi
            ei = pr * oi + pi * orr
            sums.append(
                jnp.concatenate([er[:, :half] + er[:, half:], ei[:, :half] + ei[:, half:]], 1)
            )
            differences.append(
                jnp.concatenate([er[:, :half] - er[:, half:], ei[:, :half] - ei[:, half:]], 1)
            )
        return sums, differences

    def far_field(p, te, be, to, bo):
        outs = []
        for odd, (e, o) in enumerate(((te + be, to + bo), (te - be, to - bo))):
            x = jnp.concatenate(
                [
                    jnp.concatenate([e[:, :half], o[:, :half]], 1),
                    jnp.concatenate([e[:, half:], o[:, half:]], 1),
                ],
                0,
            )
            far = times_left(mats, WO if odd else WE, x)
            fr = far[:half]
            fi = far[half:]
            amp = amps_ref[p, odd * half : (odd + 1) * half, :]
            keep = 1.0 - amp * lax.rsqrt(jnp.maximum(fr * fr + fi * fi, FLOOR * FLOOR))
            y = jnp.concatenate([fr * keep, fi * keep], 0)
            outs.append(times_left(mats, WOT if odd else WET, y))
        both = (outs[0] + outs[1], outs[0] - outs[1])
        return [
            [jnp.concatenate([v[:half, lanes], v[half:, lanes]], 1) for v in both]
            for lanes in (slice(0, half), slice(half, size))
        ]

    def place(p, e, o):
        first, second = offs_ref[0, p], offs_ref[1, p]
        for h in (0, 1):
            u = e[h] + o[h]
            w = e[h] - o[h]
            br = jnp.concatenate([u[:, :half], w[:, :half]], 1)
            bi = jnp.concatenate([u[:, half:], w[:, half:]], 1)
            pr = probe_ref[0, h * half : (h + 1) * half, :]
            pi = probe_ref[1, h * half : (h + 1) * half, :]
            rows = pl.ds(first + h * half, half)
            add_at(0, rows, pr * br + pi * bi, second)
            add_at(1, rows, pr * bi - pi * br, second)

    group = GROUP if positions % GROUP == 0 else 1
    for start in range(0, positions, group):
        ps = range(start, start + group)
        waves = [exits(p) for p in ps]
        even = halves(times_right(jnp.concatenate(sum([w[0] for w in waves], []), 0), mats, WET))
        odd = halves(times_right(jnp.concatenate(sum([w[1] for w in waves], []), 0), mats, WOT))
        backs = [
            far_field(p, *even[2 * i : 2 * i + 2], *odd[2 * i : 2 * i + 2]) for i, p in enumerate(ps)
        ]
        even = halves(times_right(jnp.concatenate(sum([b[0] for b in backs], []), 0), mats, WE))
        odd = halves(times_right(jnp.concatenate(sum([b[1] for b in backs], []), 0), mats, WO))
        for i, p in enumerate(ps):
            place(p, even[2 * i : 2 * i + 2], odd[2 * i : 2 * i + 2])
    for k in range(mid_ref.shape[0]):
        for j in range(3):
            lanes = slice(j * own, (j + 1) * own)
            mid_ref[k, :, lanes] = acc[3 * k + j, own : 2 * own, :]
            to_even_ref[k, :, lanes] = acc[3 * k + j, pl.ds(even_at, own), :]
        rows = slice(k * own, (k + 1) * own)
        for out, chunk in ((ro_ref, 1), (de_ref, even_chunk), (do_ref, odd_chunk)):
            out[rows, :] = acc[3 * k + chunk, pl.ds(odd_at, own), :]


def pack_kernel(offs_ref, field_ref, out_ref):
    own = field_ref.shape[1]
    for k in range(2):
        out_ref[k * own : (k + 1) * own, :] = field_ref[k]
    lanes = lax.broadcasted_iota(jnp.int32, (8, own), 1)
    row = jnp.zeros((8, own), jnp.int32)
    positions = offs_ref.shape[1]
    for j in range(2 * positions):
        row = jnp.where(lanes == j, offs_ref[j // positions, j % positions], row)
    out_ref[2 * own :, :] = row.astype(f32)


def light_kernel(flags_ref, offs_ref, probe_ref, light_ref, padded):
    own = light_ref.shape[0]
    size = probe_ref.shape[1]
    positions = offs_ref.shape[0] // 18
    padded[...] = jnp.zeros_like(padded)
    power = probe_ref[0] * probe_ref[0] + probe_ref[1] * probe_ref[1]
    for j in range(size // own):
        padded[1 + j, own : own + size, :] = power[:, j * own : (j + 1) * own]
    light_ref[...] = jnp.ones_like(light_ref)
    lanes = lax.broadcasted_iota(jnp.int32, (own, own), 1)
    row_step = (1 - 2 * flags_ref[0]) * own
    col_step = (1 - 2 * flags_ref[1]) * own
    for g, row in enumerate((0, row_step, -row_step)):
        for m, col in enumerate((0, col_step, -col_step)):
            for p in range(positions):
                at = 2 * (3 * g + m) * positions + p
                first = 2 * own - row - offs_ref[at]
                second = 2 * own - col - offs_ref[at + positions]

                there = is_there(flags_ref, g, m)

                @pl.when(True if there is None else there)
                def _():
                    chunk = second // own
                    by = second - chunk * own
                    back = jnp.where(by == 0, 0, own - by)
                    rows = pl.ds(first, own)
                    left = pltpu.roll(padded[chunk, rows, :], back, 1)
                    right = pltpu.roll(padded[chunk + 1, rows, :], back, 1)
                    light_ref[...] += jnp.where(lanes < own - by, left, right)


def rows_kernel(flags_ref, mid_ref, even_ref, keep_ref, to_even_ref, to_odd_ref):
    own = keep_ref.shape[1]
    col_parity = flags_ref[1]
    for k in range(2):
        rows = slice(k * own, (k + 1) * own)
        total = mid_ref[k] + even_ref[k]
        left, right = total[:, :own], total[:, 2 * own :]
        keep_ref[rows, :] = total[:, own : 2 * own]
        to_even_ref[rows, :] = jnp.where(col_parity == 0, right, left)
        to_odd_ref[rows, :] = jnp.where(col_parity == 0, left, right)


def update_kernel(
    flags_ref, field_ref, light_ref, keep_ref, ce_ref, co_ref, ro_ref, de_ref, do_ref, out_ref
):
    own = light_ref.shape[0]
    row_ok, col_ok = flags_ref[2] > 0, flags_ref[3] > 0
    light = light_ref[...]
    for k in range(2):
        rows = slice(k * own, (k + 1) * own)
        total = keep_ref[rows, :] + ce_ref[rows, :]
        total += jnp.where(col_ok, co_ref[rows, :], 0.0)
        odd_row = ro_ref[rows, :] + de_ref[rows, :] + jnp.where(col_ok, do_ref[rows, :], 0.0)
        total += jnp.where(row_ok, odd_row, 0.0)
        out_ref[rows, :] = field_ref[rows, :] - total / light


def call(kernel, shapes, specs, *args, scratch=(), flops=0):
    outs = [jax.ShapeDtypeStruct(s, f32) for s in shapes]
    moved = sum(a.size * a.dtype.itemsize for a in args)
    got = pl.pallas_call(
        kernel,
        out_shape=outs,
        in_specs=specs,
        out_specs=[VMEM] * len(outs),
        scratch_shapes=list(scratch),
        compiler_params=pltpu.CompilerParams(vmem_limit_bytes=40 * 2**20),
        cost_estimate=pl.CostEstimate(flops=flops, bytes_accessed=moved, transcendentals=0),
    )(*args)
    return got[0] if len(outs) == 1 else got


def local(object_field, probe, amplitudes, offsets):
    own = object_field.shape[1]
    size = probe.shape[1]
    positions = amplitudes.shape[2]
    extent = 3 * own
    amps = amplitudes.reshape(positions, size, size)
    offs = offsets.transpose(0, 1, 3, 2).reshape(2, positions)
    row, col = lax.axis_index("rows"), lax.axis_index("cols")
    inner = [
        (at > 0) & (at < lax.axis_size(axis) - 1) for axis, at in (("rows", row), ("cols", col))
    ]
    flags = jnp.stack([row % 2, col % 2] + [x.astype(row.dtype) for x in inner]).astype(jnp.int32)
    mats = jnp.asarray(dft_matrices(size))
    order = np.concatenate([np.arange(0, size, 2), np.arange(1, size, 2)])
    perm = (np.arange(size)[:, None] == order[None, :]).astype(jnp.bfloat16)
    perm = jnp.asarray(np.stack([perm, perm.T]))
    amps = call(
        amps_kernel, [(positions, size, size)], [VMEM, VMEM], amps, perm,
        flops=6 * positions * size**3,
    )
    field = call(
        pack_kernel, [(2 * own + 8, own)], [SMEM, VMEM], offs, object_field
    )
    tiles = halo(field)
    around = jnp.concatenate([t[2 * own, : 2 * positions] for t in tiles]).astype(jnp.int32)
    light = call(
        light_kernel, [(own, own)], [SMEM, SMEM, VMEM], flags, around, probe,
        scratch=[pltpu.VMEM((2 + size // own + 1, size + 2 * own, own), f32)],
        flops=4 * positions * size**3,
    )
    for step in range(ITERS):
        if step > 0:
            tiles = halo(field)
        mid, to_even, ro, de, do = call(
            windows_kernel,
            [(2, own, extent)] * 2 + [(2 * own, own)] * 3,
            [SMEM, SMEM] + [VMEM] * 12,
            flags, offs, *tiles, probe, amps, mats,
            scratch=[pltpu.VMEM((6, extent, own), f32)] * 2,
            flops=48 * positions * size**3,
        )
        even = swap(to_even, row=0)
        odd_row = [swap(ro, row=1), swap(de, row=1, col=0), swap(do, row=1, col=1)]
        keep, to_even, to_odd = call(
            rows_kernel, [(2 * own, own)] * 3, [SMEM] + [VMEM] * 2, flags, mid, even
        )
        co, ce = swap(to_odd, col=1), swap(to_even, col=0)
        field = call(
            update_kernel, [(2 * own, own)], [SMEM] + [VMEM] * 8,
            flags, field, light, keep, ce, co, *odd_row,
        )
    return field.reshape(2, own, own)


def solution(mesh):
    placed = (
        P(None, "rows", "cols"),
        P(),
        P("rows", "cols", None, None, None),
        P("rows", "cols", None, None),
    )

    return jax.shard_map(
        local, mesh=mesh, in_specs=placed, out_specs=P(None, "rows", "cols"), check_vma=False
    )
```
